256 devices in a mesh: blk: 64 (over x, z_lo, y), rep: 4 (over z_hi, core).
Axes of the slice: x: 4, y: 4, z: 8 (z_hi: 2, z_lo: 4; z = z_hi * 4 + z_lo), core: 2. Of those that a mesh axis runs over, the one named last changes fastest.
Arguments:
- node_feats: float32 [32768, 256], P('blk'), may hold values from -6 to 6
- operator_tiles: float32 [256, 16, 128, 128], P('blk', 'rep'), may hold values from -0.125 to 0.125
- tile_cols: int32 [256, 16], P('blk', 'rep'), may hold values from 0 to 255, as said below
- weight: float32 [256, 256], replicated, may hold values from -0.375 to 0.375
- layer_bias: float32 [256], replicated, may hold values from -3 to 3
- cotangent: float32 [32768, 256], P(('blk', 'rep')), may hold values from -6 to 6
Outputs:
- layer_out: float32 [32768, 256], P(('blk', 'rep'))
- grad_feats: float32 [32768, 256], P(('blk', 'rep'))
- grad_weight: float32 [256, 256], replicated
- grad_bias: float32 [256], replicated
The draws below stay inside these ranges and needn't reach their ends.
Inputs may be any that keep to these rules, and one draw needn't show every extreme that they name: `tile_cols`: owner of block j is j // 4, among 64 owners on a closed cycle. Slots r * 4 to (r + 1) * 4 - 1 of row block i name blocks whose owner lies at cycle distance (owner of i minus owner of the column, modulo the number of owners) from r * 16 to (r + 1) * 16 - 1. Slot 0 of row block i names block i itself. Entries may repeat within a row block.
All inputs are finite; a program needn't handle non-finite values.
Results may differ from the reference program's by a relative error of at most 0.0003.
Values sent between devices are 32-bit elements; how exact they have to be, the bound alone decides.
No kernel may reach another device: no remote copies, remote signals or barrier semaphores. Data moves between devices by JAX's collectives and lax.ppermute only.
A program may use at most 64 MiB of HBM per device.

```python
import math
import jax
import jax.numpy as jnp
from jax import lax

BS = 128
D = 256
RBD = 4
SLOTS = 4
SEG = 16
KT = 16
NB = 256
N_NODES = 32768


def draw_tile_cols(key, part):
    owner_count = NB // RBD
    row_ids = jnp.arange(NB, dtype=jnp.int32)
    slot_indices = jnp.arange(KT, dtype=jnp.int32)
    key_dist, key_within = jax.random.split(key)
    offsets = jax.random.randint(key_dist, (NB, KT), 0, SEG, dtype=jnp.int32)
    distance = (slot_indices // SLOTS)[None, :] * SEG + offsets
    within = jax.random.randint(key_within, (NB, KT), 0, RBD, dtype=jnp.int32)
    column_owner = jnp.mod(row_ids[:, None] // RBD - distance, owner_count)
    columns = column_owner * RBD + within
    return columns.at[:, 0].set(row_ids)


def steps_of(key, shape, pieces, smallest, top_value):
    def one(position, shards_of):
        heights = jax.random.uniform(jax.random.fold_in(jax.random.fold_in(key, 6), position), (shards_of,), jnp.float32, smallest / len(pieces), top_value / len(pieces))
        return jnp.repeat(jnp.exp(heights), shape[position] // shards_of).reshape((-1,) + (1,) * (len(shape) - position - 1))

    factor_of = one(*pieces[0])
    for cut in pieces[1:]:
        factor_of = factor_of * one(*cut)
    return factor_of


def bell_draw(rng, dims, spread, limit, cuts=(), kind=jnp.bfloat16):
    result = spread * jax.random.normal(rng, dims, jnp.float32)
    if cuts:
        result = result * steps_of(rng, dims, cuts, -0.22, 0.18)
    return jnp.clip(result, -limit, limit).astype(kind)


def setup_inputs(seed: int = 0) -> dict:
    streams_of = jax.random.split(jax.random.key(seed), 7)
    node_feats = bell_draw(streams_of[0], (N_NODES, D), 1.0, 6.0, ((0, 64),), jnp.float32)
    operator_tiles = bell_draw(streams_of[1], (NB, KT, BS, BS), (BS * KT) ** -0.5, 0.125, ((0, 64), (1, 4)), jnp.float32)
    tile_cols = draw_tile_cols(jax.random.fold_in(streams_of[6], 71), 0)
    weight = bell_draw(streams_of[3], (D, D), D ** -0.5, 0.375, (), jnp.float32)
    layer_bias = bell_draw(streams_of[4], (D,), 0.5, 3.0, (), jnp.float32)
    cotangent = bell_draw(streams_of[5], (N_NODES, D), 1.0, 6.0, ((0, 256),), jnp.float32)
    return dict(node_feats=node_feats, operator_tiles=operator_tiles, tile_cols=tile_cols, weight=weight, layer_bias=layer_bias, cotangent=cotangent)


TOP_PRECISION = lax.Precision.HIGHEST

def reference(node_feats, operator_tiles, tile_cols, weight, layer_bias, cotangent):
    blocks_in = node_feats.reshape(NB, BS, D)

    def aggregate_row(pair):
        tile_set, column_ids = pair
        gathered = blocks_in[column_ids]
        return jnp.einsum('kab,kbd->ad', tile_set, gathered, precision=TOP_PRECISION)
    hidden = lax.map(aggregate_row, (operator_tiles, tile_cols)).reshape(N_NODES, D)
    pre_act = jnp.dot(hidden, weight, precision=TOP_PRECISION) + layer_bias
    negative = jnp.minimum(pre_act, 0.0)
    layer_out = jnp.where(pre_act > 0, pre_act, jnp.expm1(negative))
    grad_pre = cotangent * jnp.where(pre_act > 0, 1.0, jnp.exp(negative))
    grad_scale = 1.0 / math.sqrt(N_NODES)
    grad_weight = jnp.dot(hidden.T, grad_pre, precision=TOP_PRECISION) * grad_scale
    grad_bias = lax.optimization_barrier(jnp.sum(grad_pre, axis=0)) * grad_scale
    grad_hidden = jnp.dot(grad_pre, weight.T, precision=TOP_PRECISION).reshape(NB, BS, D)

    def scatter_row(accum, triple):
        tile_set, column_ids, rows_grad = triple
        terms = jnp.einsum('kab,ad->kbd', tile_set, rows_grad, precision=TOP_PRECISION)
        return (accum.at[column_ids].add(terms), None)
    grad_blocks, _ = lax.scan(scatter_row, jnp.zeros((NB, BS, D), node_feats.dtype), (operator_tiles, tile_cols, grad_hidden))
    return (layer_out, grad_blocks.reshape(N_NODES, D), grad_weight, grad_bias)
```

```python
import math

import jax
import jax.numpy as jnp
from jax import lax
from jax.experimental import pallas as pl
from jax.experimental.pallas import tpu as pltpu
from jax.sharding import Mesh
from jax.sharding import PartitionSpec as P

AXES = ("x", "zl", "y", "zh", "c")
PLANE = ("zl", "y")
TOP = lax.Precision.HIGHEST
F32 = jnp.float32
LIMIT = 48 * 1024 * 1024


def shift(value, axis, steps):
    count = lax.axis_size(axis)
    return lax.ppermute(value, axis, [(s, (s + steps) % count) for s in range(count)])


def plane_exchange(value):
    return lax.all_to_all(value, PLANE, 0, 0, tiled=True)


def vmem():
    return pl.BlockSpec(memory_space=pltpu.VMEM)


def smem():
    return pl.BlockSpec(memory_space=pltpu.SMEM)


def call(kernel, out_shape, specs, scratch=(), flops=0, moved=0):
    return pl.pallas_call(
        kernel,
        out_shape=out_shape,
        in_specs=specs,
        out_specs=jax.tree.map(lambda _: vmem(), out_shape),
        scratch_shapes=scratch,
        compiler_params=pltpu.CompilerParams(vmem_limit_bytes=LIMIT),
        cost_estimate=pl.CostEstimate(flops=flops, bytes_accessed=moved, transcendentals=0),
    )


def gather_kernel(index_ref, where_ref, near_ref, far_ref, out_ref):
    core = where_ref[0]

    def one(dest, carry):
        for slot in range(16):
            row = index_ref[dest * 16 + slot]
            out_ref[dest, 2 * slot + core] = near_ref[row]
            out_ref[dest, 2 * slot + 1 - core] = far_ref[row]
        return carry

    lax.fori_loop(0, 16, one, 0)


def scatter_kernel(index_ref, where_ref, got_ref, keep_ref, send_ref):
    core = where_ref[0]
    keep_ref[...] = jnp.zeros_like(keep_ref)
    send_ref[...] = jnp.zeros_like(send_ref)

    def one(source, carry):
        for slot in range(16):
            row = index_ref[source * 16 + slot]
            spot = row + 6 * (row // 64)
            keep_ref[spot] += got_ref[source, 2 * slot + core]
            send_ref[spot] += got_ref[source, 2 * slot + 1 - core]
        return carry

    lax.fori_loop(0, 16, one, 0)
    for part in range(6):
        total = jnp.sum(got_ref[:, 32 + part], axis=0)
        for plane in range(4):
            keep_ref[plane * 70 + 64 + part] = total
            send_ref[plane * 70 + 64 + part] = total


def dot(a, b):
    return lax.dot_general(
        a, b, (((1,), (0,)), ((), ())), precision=TOP, preferred_element_type=F32
    )


def dot_first(a, b):
    return lax.dot_general(
        a, b, (((0,), (0,)), ((), ())), precision=TOP, preferred_element_type=F32
    )


def dot_last(a, b):
    return lax.dot_general(
        a, b, (((1,), (1,)), ((), ())), precision=TOP, preferred_element_type=F32
    )


def forward_kernel(where_ref, own_ref, swapped_ref, got_ref, out_ref):
    half = where_ref[1]
    for block in range(2):
        total = [jnp.zeros((128, 128), F32), jnp.zeros((128, 128), F32)]
        for source in range(2):
            for k in range(4):
                slot = block * 8 + source * 4 + k
                tile = own_ref[2 * half + block, k] if source == 0 else swapped_ref[block, k]
                for h in range(2):
                    total[h] += dot(tile, got_ref[:, 2 * slot + h].reshape(128, 128))
        for h in range(2):
            out_ref[block, :, 128 * h : 128 * (h + 1)] = total[h]


def middle_kernel(
    scale,
    where_ref,
    own_ref,
    swapped_ref,
    mine_ref,
    other_ref,
    cot_ref,
    weight_ref,
    bias_ref,
    layer_ref,
    out_ref,
):
    core = where_ref[0]
    half = where_ref[1]
    for block in range(2):
        hidden = mine_ref[block] + other_ref[block]
        pre = dot(hidden, weight_ref[...]) + bias_ref[...]
        grow = jnp.exp(jnp.minimum(pre, 0.0))
        layer = jnp.where(pre > 0, pre, grow - 1.0)
        grad_pre = cot_ref[block] * jnp.where(pre > 0, 1.0, grow)
        grad_hidden = dot_last(grad_pre, weight_ref[...])

        @pl.when(core == block)
        def _():
            layer_ref[...] = layer
            grad_weight = dot_first(hidden, grad_pre) * scale
            grad_bias = jnp.sum(grad_pre, axis=0, keepdims=True) * scale
            for m in range(16):
                for part in range(4):
                    top, left = 16 * m + 8 * (part // 2), 128 * (part % 2)
                    out_ref[m, 32 + part] = grad_weight[top : top + 8, left : left + 128]
                for h in range(2):
                    out_ref[m, 36 + h] = jnp.broadcast_to(
                        grad_bias[:, 128 * h : 128 * (h + 1)], (8, 128)
                    )

        for source in range(2):
            for k in range(4):
                slot = block * 8 + source * 4 + k
                tile = own_ref[2 * half + block, k] if source == 0 else swapped_ref[block, k]
                term = dot_first(tile, grad_hidden)
                for h in range(2):
                    out_ref[:, 2 * slot + h] = term[:, 128 * h : 128 * (h + 1)].reshape(
                        16, 8, 128
                    )


def body(node_feats, operator_tiles, tile_cols, weight, layer_bias, cotangent):
    x = lax.axis_index("x")
    half = lax.axis_index("zh")
    core = lax.axis_index("c")
    where = jnp.stack([core, half]).astype(jnp.int32)
    scale = 1.0 / math.sqrt(32768)

    swapped = shift(lax.dynamic_slice_in_dim(operator_tiles, 2 * (1 - half), 2, 0), "zh", 1)
    cot_other = shift(cotangent, "c", 1)
    cots = jnp.where(
        core == 0, jnp.stack([cotangent, cot_other]), jnp.stack([cot_other, cotangent])
    )

    columns = lax.dynamic_slice_in_dim(node_feats, core * 128, 128, 1)
    chunks = columns.reshape(4, 16, 8, 128).transpose(1, 0, 2, 3)
    wanted = jnp.pad(tile_cols.astype(F32).reshape(1, 16), ((0, 7), (0, 112)))
    wanted = jnp.broadcast_to(wanted[None, None], (16, 1, 8, 128))
    arrived = plane_exchange(jnp.concatenate([chunks, wanted], axis=1))
    plane = arrived[:, :4].reshape(64, 8, 128)
    near = jnp.concatenate([plane] + [shift(plane, "x", d) for d in (1, 2, 3)], axis=0)
    far = shift(near, "c", 1)

    asked = arrived[:, 4, 0, :16]
    asked_other = shift(asked, "zh", 1)
    asked = jnp.stack([asked.reshape(16, 4, 4), asked_other.reshape(16, 4, 4)], axis=2)
    asked = lax.dynamic_slice_in_dim(asked, 2 * half, 2, 1).reshape(256).astype(jnp.int32)
    index = jnp.mod(x - asked // 64, 4) * 64 + asked % 64

    sent = call(
        gather_kernel,
        jax.ShapeDtypeStruct((16, 32, 8, 128), F32),
        [smem(), smem(), vmem(), vmem()],
        moved=4 << 20,
    )(index, where, near, far)
    got = plane_exchange(sent)
    mine = call(
        forward_kernel,
        jax.ShapeDtypeStruct((2, 128, 256), F32),
        [smem(), vmem(), vmem(), vmem()],
        flops=134217728 * 6,
        moved=4 << 20,
    )(where, operator_tiles, swapped, got)
    other = shift(mine, "c", 1)

    def middle(*refs):
        middle_kernel(scale, *refs)

    layer_out, terms = call(
        middle,
        (
            jax.ShapeDtypeStruct((128, 256), F32),
            jax.ShapeDtypeStruct((16, 38, 8, 128), F32),
        ),
        [smem()] + [vmem()] * 7,
        flops=234217728 * 6,
        moved=5 << 20,
    )(where, operator_tiles, swapped, mine, other, cots, weight, layer_bias.reshape(1, 256))
    back = plane_exchange(terms)
    keep, send = call(
        scatter_kernel,
        (
            jax.ShapeDtypeStruct((280, 8, 128), F32),
            jax.ShapeDtypeStruct((280, 8, 128), F32),
        ),
        [smem(), smem(), vmem()],
        moved=5 << 20,
    )(index, where, back)
    table = (keep + shift(send, "c", 1)).reshape(4, 70, 8, 128)
    total = table[0]
    for d in (1, 2, 3):
        total = total + shift(table[d], "x", -d)
    by_owner = total[:64].reshape(16, 4, 8, 128)
    staying = lax.dynamic_slice_in_dim(by_owner, 2 * half, 2, 1).reshape(32, 8, 128)
    leaving = lax.dynamic_slice_in_dim(by_owner, 2 * (1 - half), 2, 1).reshape(32, 8, 128)
    final = jnp.concatenate([staying, total[64:]], axis=0) + shift(
        jnp.concatenate([leaving, total[64:]], axis=0), "zh", 1
    )
    home = plane_exchange(
        jnp.concatenate(
            [
                final[:32].reshape(16, 2, 8, 128),
                jnp.broadcast_to(final[None, 32:36], (16, 4, 8, 128)),
            ],
            axis=1,
        )
    )
    grad_weight = (
        home[:, 2:].reshape(16, 2, 2, 8, 128).transpose(0, 1, 3, 2, 4).reshape(256, 256)
    )
    grad_bias = final[36:, 0].reshape(256)
    pair = home[:, :2].transpose(1, 0, 2, 3).reshape(2, 128, 128)
    own = lax.dynamic_index_in_dim(pair, core, 0, keepdims=False)
    given = shift(lax.dynamic_index_in_dim(pair, 1 - core, 0, keepdims=False), "c", 1)
    grad_feats = jnp.where(
        core == 0,
        jnp.concatenate([own, given], axis=1),
        jnp.concatenate([given, own], axis=1),
    )
    return layer_out, grad_feats, grad_weight, grad_bias


def solution(mesh):
    fine = Mesh(mesh.devices.reshape(4, 4, 4, 2, 2), AXES)
    blk, rep = ("x", "zl", "y"), ("zh", "c")
    return jax.shard_map(
        body,
        mesh=fine,
        in_specs=(
            P(blk, None),
            P(blk, rep, None, None),
            P(blk, rep),
            P(),
            P(),
            P(AXES, None),
        ),
        out_specs=(P(AXES, None), P(AXES, None), P(), P()),
        check_vma=False,
    )
```

```python
import math

import jax
import jax.numpy as jnp
from jax import lax
from jax.experimental import pallas as pl
from jax.experimental.pallas import tpu as pltpu
from jax.sharding import Mesh
from jax.sharding import PartitionSpec as P

AXES = ("x", "zl", "y", "zh", "c")
PLANE = ("x", "y")
TOP = lax.Precision.HIGHEST
F32 = jnp.float32
LIMIT = 48 * 1024 * 1024


def shift(value, axis, steps):
    count = lax.axis_size(axis)
    return lax.ppermute(value, axis, [(s, (s + steps) % count) for s in range(count)])


def ring(value, steps):
    pairs = []
    for s in range(8):
        d = (s + steps) % 8
        pairs.append(((s % 4) * 2 + s // 4, (d % 4) * 2 + d // 4))
    return lax.ppermute(value, ("zl", "zh"), pairs)


def plane_exchange(value):
    return lax.all_to_all(value, PLANE, 0, 0, tiled=True)


def vmem():
    return pl.BlockSpec(memory_space=pltpu.VMEM)


def smem():
    return pl.BlockSpec(memory_space=pltpu.SMEM)


def call(kernel, out_shape, specs, scratch=(), flops=0, moved=0):
    return pl.pallas_call(
        kernel,
        out_shape=out_shape,
        in_specs=specs,
        out_specs=jax.tree.map(lambda _: vmem(), out_shape),
        scratch_shapes=scratch,
        compiler_params=pltpu.CompilerParams(vmem_limit_bytes=LIMIT),
        cost_estimate=pl.CostEstimate(flops=flops, bytes_accessed=moved, transcendentals=0),
    )


def gather_kernel(index_ref, where_ref, near_ref, far_ref, out_ref):
    core = where_ref[0]

    def one(dest, carry):
        for slot in range(16):
            row = index_ref[dest * 16 + slot]
            out_ref[dest, 2 * slot + core] = near_ref[row]
            out_ref[dest, 2 * slot + 1 - core] = far_ref[row]
        return carry

    lax.fori_loop(0, 16, one, 0)


def scatter_kernel(index_ref, where_ref, got_ref, keep_ref, send_ref):
    core = where_ref[0]
    keep_ref[...] = jnp.zeros_like(keep_ref)
    send_ref[...] = jnp.zeros_like(send_ref)

    def one(source, carry):
        for slot in range(16):
            row = index_ref[source * 16 + slot]
            spot = row + 6 * (row // 64) + 6
            keep_ref[spot] += got_ref[source, 2 * slot + core]
            send_ref[spot] += got_ref[source, 2 * slot + 1 - core]
        return carry

    lax.fori_loop(0, 16, one, 0)
    for part in range(6):
        total = jnp.sum(got_ref[:, 32 + part], axis=0)
        for plane in range(4):
            keep_ref[plane * 70 + part] = total
            send_ref[plane * 70 + part] = total


def dot(a, b):
    return lax.dot_general(
        a, b, (((1,), (0,)), ((), ())), precision=TOP, preferred_element_type=F32
    )


def dot_first(a, b):
    return lax.dot_general(
        a, b, (((0,), (0,)), ((), ())), precision=TOP, preferred_element_type=F32
    )


def dot_last(a, b):
    return lax.dot_general(
        a, b, (((1,), (1,)), ((), ())), precision=TOP, preferred_element_type=F32
    )


def forward_kernel(where_ref, own_ref, first_ref, second_ref, got_ref, out_ref):
    swapped = (first_ref, second_ref)
    half = where_ref[1]
    for block in range(2):
        total = [jnp.zeros((128, 128), F32), jnp.zeros((128, 128), F32)]
        for source in range(2):
            for k in range(4):
                slot = block * 8 + source * 4 + k
                tile = own_ref[2 * half + block, k] if source == 0 else swapped[block][k]
                for h in range(2):
                    total[h] += dot(tile, got_ref[:, 2 * slot + h].reshape(128, 128))
        for h in range(2):
            out_ref[block, :, 128 * h : 128 * (h + 1)] = total[h]


def middle_kernel(
    scale,
    where_ref,
    own_ref,
    first_ref,
    second_ref,
    mine_ref,
    other_ref,
    cot_ref,
    weight_ref,
    bias_ref,
    layer_ref,
    out_ref,
):
    core = where_ref[0]
    half = where_ref[1]
    swapped = (first_ref, second_ref)
    for block in range(2):
        hidden = mine_ref[block] + other_ref[block]
        pre = dot(hidden, weight_ref[...]) + bias_ref[...]
        grow = jnp.exp(jnp.minimum(pre, 0.0))
        layer = jnp.where(pre > 0, pre, grow - 1.0)
        grad_pre = cot_ref[block] * jnp.where(pre > 0, 1.0, grow)
        grad_hidden = dot_last(grad_pre, weight_ref[...])

        @pl.when(core == block)
        def _():
            layer_ref[...] = layer
            grad_weight = dot_first(hidden, grad_pre) * scale
            grad_bias = jnp.sum(grad_pre, axis=0, keepdims=True) * scale
            for m in range(16):
                for part in range(4):
                    top, left = 16 * m + 8 * (part // 2), 128 * (part % 2)
                    out_ref[m, 32 + part] = grad_weight[top : top + 8, left : left + 128]
                for h in range(2):
                    out_ref[m, 36 + h] = jnp.broadcast_to(
                        grad_bias[:, 128 * h : 128 * (h + 1)], (8, 128)
                    )

        for source in range(2):
            for k in range(4):
                slot = block * 8 + source * 4 + k
                tile = own_ref[2 * half + block, k] if source == 0 else swapped[block][k]
                term = dot_first(tile, grad_hidden)
                for h in range(2):
                    out_ref[:, 2 * slot + h] = term[:, 128 * h : 128 * (h + 1)].reshape(
                        16, 8, 128
                    )


def body(node_feats, operator_tiles, tile_cols, weight, layer_bias, cotangent):
    level = lax.axis_index("zl")
    half = lax.axis_index("zh")
    core = lax.axis_index("c")
    where = jnp.stack([core, half]).astype(jnp.int32)
    scale = 1.0 / math.sqrt(32768)

    def theirs(block):
        return lax.dynamic_index_in_dim(operator_tiles, 2 * (1 - half) + block, 0, keepdims=False)

    first = shift(theirs(0), "zh", 1)
    cot_other = shift(cotangent, "c", 1)
    cots = jnp.where(
        core == 0, jnp.stack([cotangent, cot_other]), jnp.stack([cot_other, cotangent])
    )

    columns = lax.dynamic_slice_in_dim(node_feats, core * 128, 128, 1)
    chunks = columns.reshape(4, 16, 8, 128).transpose(1, 0, 2, 3)
    wanted = jnp.pad(tile_cols.astype(F32).reshape(1, 16), ((0, 7), (0, 112)))
    wanted = jnp.broadcast_to(wanted[None, None], (16, 1, 8, 128))
    arrived = plane_exchange(jnp.concatenate([chunks, wanted], axis=1))
    arrived, first = lax.optimization_barrier((arrived, first))
    plane = arrived[:, :4].reshape(64, 8, 128)
    near = jnp.concatenate(
        [plane, ring(plane, -1), ring(plane[:32], -2), ring(plane[32:], 2), ring(plane, 1)], axis=0
    )
    near, leaving = lax.optimization_barrier((near, theirs(1)))
    second = shift(leaving, "zh", 1)
    far = shift(near, "c", 1)

    asked = arrived[:, 4, 0, :16]
    asked_other = shift(asked, "zh", 1)
    asked = jnp.stack([asked.reshape(16, 4, 4), asked_other.reshape(16, 4, 4)], axis=2)
    asked = lax.dynamic_slice_in_dim(asked, 2 * half, 2, 1).reshape(256).astype(jnp.int32)
    owner = asked // 4
    spot = (owner // 16 * 4 + owner % 4) * 4 + asked % 4
    index = jnp.mod(owner // 4 % 4 - level, 4) * 64 + spot

    sent = call(
        gather_kernel,
        jax.ShapeDtypeStruct((16, 32, 8, 128), F32),
        [smem(), smem(), vmem(), vmem()],
        moved=4 << 20,
    )(index, where, near, far)
    got = plane_exchange(sent)
    mine = call(
        forward_kernel,
        jax.ShapeDtypeStruct((2, 128, 256), F32),
        [smem(), vmem(), vmem(), vmem(), vmem()],
        flops=134217728 * 6,
        moved=4 << 20,
    )(where, operator_tiles, first, second, got)
    other = shift(mine, "c", 1)

    def middle(*refs):
        middle_kernel(scale, *refs)

    layer_out, terms = call(
        middle,
        (
            jax.ShapeDtypeStruct((128, 256), F32),
            jax.ShapeDtypeStruct((16, 38, 8, 128), F32),
        ),
        [smem()] + [vmem()] * 8,
        flops=234217728 * 6,
        moved=5 << 20,
    )(where, operator_tiles, first, second, mine, other, cots, weight, layer_bias.reshape(1, 256))
    back = plane_exchange(terms)
    keep, send = call(
        scatter_kernel,
        (
            jax.ShapeDtypeStruct((280, 8, 128), F32),
            jax.ShapeDtypeStruct((280, 8, 128), F32),
        ),
        [smem(), smem(), vmem()],
        moved=5 << 20,
    )(index, where, back)
    table = (keep + shift(send, "c", 1)).reshape(4, 70, 8, 128)
    total = table[0] + ring(table[1], 1) + ring(table[3], -1)
    total = total + jnp.concatenate([ring(table[2, :38], 2), ring(table[2, 38:], -2)], axis=0)
    by_owner = total[6:].reshape(16, 4, 8, 128)
    staying = lax.dynamic_slice_in_dim(by_owner, 2 * half, 2, 1).reshape(32, 8, 128)
    leaving = lax.dynamic_slice_in_dim(by_owner, 2 * (1 - half), 2, 1).reshape(32, 8, 128)
    final = jnp.concatenate([staying, total[:6]], axis=0) + shift(
        jnp.concatenate([leaving, total[:6]], axis=0), "zh", 1
    )
    home = plane_exchange(
        jnp.concatenate(
            [
                final[:32].reshape(16, 2, 8, 128),
                jnp.broadcast_to(final[None, 32:36], (16, 4, 8, 128)),
            ],
            axis=1,
        )
    )
    grad_weight = (
        home[:, 2:].reshape(16, 2, 2, 8, 128).transpose(0, 1, 3, 2, 4).reshape(256, 256)
    )
    grad_bias = final[36:, 0].reshape(256)
    pair = home[:, :2].transpose(1, 0, 2, 3).reshape(2, 128, 128)
    own = lax.dynamic_index_in_dim(pair, core, 0, keepdims=False)
    given = shift(lax.dynamic_index_in_dim(pair, 1 - core, 0, keepdims=False), "c", 1)
    grad_feats = jnp.where(
        core == 0,
        jnp.concatenate([own, given], axis=1),
        jnp.concatenate([given, own], axis=1),
    )
    return layer_out, grad_feats, grad_weight, grad_bias


def solution(mesh):
    fine = Mesh(mesh.devices.reshape(4, 4, 4, 2, 2), AXES)
    blk, rep = ("x", "zl", "y"), ("zh", "c")
    return jax.shard_map(
        body,
        mesh=fine,
        in_specs=(
            P(blk, None),
            P(blk, rep, None, None),
            P(blk, rep),
            P(),
            P(),
            P(AXES, None),
        ),
        out_specs=(P(AXES, None), P(AXES, None), P(), P()),
        check_vma=False,
    )
```

```python
import math

import jax
import jax.numpy as jnp
from jax import lax
from jax.experimental import pallas as pl
from jax.experimental.pallas import tpu as pltpu
from jax.sharding import Mesh
from jax.sharding import PartitionSpec as P

AXES = ("x", "zl", "y", "zh", "c")
PLANE = ("x", "y")
GROUP = ("x", "y", "c")
TOP = lax.Precision.HIGHEST
F32 = jnp.float32
LIMIT = 10 * 1024 * 1024


def shift(value, axis, steps):
    count = lax.axis_size(axis)
    return lax.ppermute(value, axis, [(s, (s + steps) % count) for s in range(count)])


def ring(value, steps):
    pairs = []
    for s in range(8):
        d = (s + steps) % 8
        pairs.append(((s % 4) * 2 + s // 4, (d % 4) * 2 + d // 4))
    return lax.ppermute(value, ("zl", "zh"), pairs)


def exchange(value, axes):
    return lax.all_to_all(value, axes, 0, 0, tiled=True)


def vmem():
    return pl.BlockSpec(memory_space=pltpu.VMEM)


def smem():
    return pl.BlockSpec(memory_space=pltpu.SMEM)


def call(kernel, out_shape, specs, scratch=(), flops=0, moved=0):
    return pl.pallas_call(
        kernel,
        out_shape=out_shape,
        in_specs=specs,
        out_specs=jax.tree.map(lambda _: vmem(), out_shape),
        scratch_shapes=scratch,
        compiler_params=pltpu.CompilerParams(vmem_limit_bytes=LIMIT),
        cost_estimate=pl.CostEstimate(flops=flops, bytes_accessed=moved, transcendentals=0),
    )


def pack_kernel(where_ref, rows_ref, wanted_ref, out_ref):
    for h in range(2):

        @pl.when(where_ref[0] == h)
        def _():
            for b in range(4):
                half = rows_ref[128 * b : 128 * (b + 1), 128 * h : 128 * (h + 1)]
                out_ref[:, b] = half.reshape(16, 8, 128)

    out_ref[:, 4] = jnp.broadcast_to(wanted_ref[...].reshape(1, 1, 128), (16, 8, 128))


def row_of(near_ref, far_ref, q, c, slot):
    block, source, k = slot // 8, slot // 4 % 2, slot % 4
    index_ref = far_ref if source else near_ref
    return index_ref[q, 16 * c + 8 * source + 4 * block + k]


def gather_kernel(near_ref, far_ref, table_ref, out_ref):
    def one(q, carry):
        for c in range(2):
            for slot in range(16):
                row = row_of(near_ref, far_ref, q, c, slot)
                out_ref[q * 2 + c, slot] = table_ref[row]
        return carry

    lax.fori_loop(0, 16, one, 0)


def scatter_kernel(near_ref, far_ref, got_ref, out_ref, even_ref, odd_ref):
    even_ref[...] = jnp.zeros_like(even_ref)
    odd_ref[...] = jnp.zeros_like(odd_ref)

    def one(q, carry):
        for slot in range(16):
            even_ref[row_of(near_ref, far_ref, q, 0, slot)] += got_ref[q, 0, slot]
            odd_ref[row_of(near_ref, far_ref, q, 1, slot)] += got_ref[q, 1, slot]
        return carry

    lax.fori_loop(0, 16, one, 0)
    sums = [
        jnp.sum(got_ref[:, 0, 16], axis=0),
        jnp.sum(got_ref[:, 1, 16], axis=0),
        jnp.sum(got_ref[:, 0, 17] + got_ref[:, 1, 17], axis=0),
    ]
    for plane in range(4):
        for part in range(3):
            out_ref[plane, part] = sums[part]
        rows = pl.ds(plane * 64, 64)
        out_ref[plane, 3:67] = even_ref[rows] + odd_ref[rows]


def dot(a, b):
    return lax.dot_general(
        a, b, (((1,), (0,)), ((), ())), precision=TOP, preferred_element_type=F32
    )


def dot_first(a, b):
    return lax.dot_general(
        a, b, (((0,), (0,)), ((), ())), precision=TOP, preferred_element_type=F32
    )


def dot_last(a, b):
    return lax.dot_general(
        a, b, (((1,), (1,)), ((), ())), precision=TOP, preferred_element_type=F32
    )


def tile_of(half, refs, block, source, k):
    own_ref, first_ref, second_ref = refs
    place = 4 * block + k
    if source == 0:
        return own_ref[8 * half + place]
    return first_ref[place] if place < 2 else second_ref[place - 2]


def forward_kernel(where_ref, own_ref, first_ref, second_ref, got_ref, out_ref):
    half = where_ref[1]
    for block in range(2):
        total = [jnp.zeros((128, 128), F32), jnp.zeros((128, 128), F32)]
        for source in range(2):
            for k in range(4):
                slot = block * 8 + source * 4 + k
                tile = tile_of(half, (own_ref, first_ref, second_ref), block, source, k)
                for h in range(2):
                    total[h] += dot(tile, got_ref[:, h, slot].reshape(128, 128))
        for h in range(2):
            out_ref[block, :, 128 * h : 128 * (h + 1)] = total[h]


def middle_kernel(
    scale,
    where_ref,
    own_ref,
    first_ref,
    second_ref,
    mine_ref,
    other_ref,
    cot_ref,
    cot_other_ref,
    weight_ref,
    bias_ref,
    layer_ref,
    out_ref,
):
    core = where_ref[0]
    half = where_ref[1]
    hiddens = []
    grads = []
    for block in range(2):
        hidden = mine_ref[block] + other_ref[block]
        pre = dot(hidden, weight_ref[...]) + bias_ref[...]
        grow = jnp.exp(jnp.minimum(pre, 0.0))
        layer = jnp.where(pre > 0, pre, grow - 1.0)
        cot = jnp.where(core == block, cot_ref[...], cot_other_ref[...])
        grad_pre = cot * jnp.where(pre > 0, 1.0, grow)
        grad_hidden = dot_last(grad_pre, weight_ref[...])
        hiddens.append(hidden)
        grads.append(grad_pre)

        @pl.when(core == block)
        def _():
            layer_ref[...] = layer

        for source in range(2):
            for k in range(4):
                slot = block * 8 + source * 4 + k
                tile = tile_of(half, (own_ref, first_ref, second_ref), block, source, k)
                term = dot_first(tile, grad_hidden)
                for h in range(2):
                    out_ref[:, h, slot] = term[:, 128 * h : 128 * (h + 1)].reshape(16, 8, 128)

    for h in range(2):

        @pl.when(core == h)
        def _():
            columns = slice(128 * h, 128 * (h + 1))
            grad_weight = dot_first(hiddens[0], grads[0][:, columns])
            grad_weight = (grad_weight + dot_first(hiddens[1], grads[1][:, columns])) * scale
            out_ref[:, :, 16] = grad_weight.reshape(16, 2, 8, 128)
            both = grads[0][:, columns] + grads[1][:, columns]
            grad_bias = jnp.sum(both, axis=0, keepdims=True) * scale
            rows = lax.broadcasted_iota(jnp.int32, (8, 128), 0)
            grad_bias = jnp.where(rows == h, jnp.broadcast_to(grad_bias, (8, 128)), 0.0)
            out_ref[:, :, 17] = jnp.broadcast_to(grad_bias.reshape(1, 1, 8, 128), (16, 2, 8, 128))


def body(node_feats, operator_tiles, tile_cols, weight, layer_bias, cotangent):
    level = lax.axis_index("zl")
    half = lax.axis_index("zh")
    core = lax.axis_index("c")
    where = jnp.stack([core, half]).astype(jnp.int32)
    scale = 1.0 / math.sqrt(32768)

    tiles = operator_tiles.reshape(16, 128, 128)
    first = shift(lax.dynamic_slice_in_dim(tiles, 8 * (1 - half), 2, 0), "zh", 1)
    cot_other = shift(cotangent, "c", 1)

    asked = tile_cols.reshape(2, 8)
    owner = asked // 4
    spot = (owner // 16 * 4 + owner % 4) * 4 + asked % 4
    asked = jnp.mod(owner // 4 % 4 - level, 4) * 64 + spot
    asked = jnp.where(half == 0, asked, asked[::-1]).astype(F32).reshape(1, 16)
    beside = shift(asked, "c", 1)
    wanted = jnp.where(
        core == 0,
        jnp.concatenate([asked, beside], axis=1),
        jnp.concatenate([beside, asked], axis=1),
    )
    wanted = jnp.pad(wanted, ((0, 0), (0, 96)))

    packed = call(
        pack_kernel,
        jax.ShapeDtypeStruct((16, 5, 8, 128), F32),
        [smem(), vmem(), vmem()],
        moved=1 << 20,
    )(where, node_feats, wanted)
    arrived = exchange(packed, PLANE)
    plane = arrived[:, :4].reshape(64, 8, 128)
    table = jnp.concatenate(
        [plane, ring(plane, -1), ring(plane[:32], -2), ring(plane[32:], 2), ring(plane, 1)], axis=0
    )
    asked = arrived[:, 4, 0]
    index = (asked.astype(jnp.int32), shift(asked, "zh", 1).astype(jnp.int32))

    table, leaving = lax.optimization_barrier(
        (table, lax.dynamic_slice_in_dim(tiles, 8 * (1 - half) + 2, 6, 0))
    )
    second = shift(leaving, "zh", 1)
    sent = call(
        gather_kernel,
        jax.ShapeDtypeStruct((32, 16, 8, 128), F32),
        [smem(), smem(), vmem()],
        moved=3 << 20,
    )(*index, table)
    sent, first = lax.optimization_barrier((sent, first))
    got = exchange(sent, GROUP).reshape(16, 2, 16, 8, 128)
    mine = call(
        forward_kernel,
        jax.ShapeDtypeStruct((2, 128, 256), F32),
        [smem()] + [vmem()] * 4,
        flops=134217728 * 6,
        moved=3 << 20,
    )(where, tiles, first, second, got)
    other = shift(mine, "c", 1)

    def middle(*refs):
        middle_kernel(scale, *refs)

    layer_out, terms = call(
        middle,
        (
            jax.ShapeDtypeStruct((128, 256), F32),
            jax.ShapeDtypeStruct((16, 2, 18, 8, 128), F32),
        ),
        [smem()] + [vmem()] * 9,
        flops=234217728 * 6,
        moved=4 << 20,
    )(where, tiles, first, second, mine, other, cotangent, cot_other, weight, layer_bias.reshape(1, 256))
    back = exchange(terms.reshape(32, 18, 8, 128), GROUP).reshape(16, 2, 18, 8, 128)
    sums = call(
        scatter_kernel,
        jax.ShapeDtypeStruct((4, 67, 8, 128), F32),
        [smem(), smem(), vmem()],
        scratch=[pltpu.VMEM((256, 8, 128), F32)] * 2,
        moved=4 << 20,
    )(*index, back)
    total = sums[0] + ring(sums[1], 1) + ring(sums[3], -1)
    total = total + jnp.concatenate([ring(sums[2, :35], 2), ring(sums[2, 35:], -2)], axis=0)
    by_owner = total[3:].reshape(16, 4, 8, 128)
    staying = lax.dynamic_slice_in_dim(by_owner, 2 * half, 2, 1).reshape(32, 8, 128)
    leaving = lax.dynamic_slice_in_dim(by_owner, 2 * (1 - half), 2, 1).reshape(32, 8, 128)
    final = jnp.concatenate([staying, total[:3]], axis=0) + shift(
        jnp.concatenate([leaving, total[:3]], axis=0), "zh", 1
    )
    home = exchange(
        jnp.concatenate(
            [
                final[:32, None],
                jnp.broadcast_to(final[None, 32:34], (32, 2, 8, 128)),
            ],
            axis=1,
        ),
        GROUP,
    ).reshape(16, 2, 3, 8, 128)
    grad_feats = home[:, :, 0].transpose(0, 2, 1, 3).reshape(128, 256)
    grad_weight = home[:, :, 1:].transpose(0, 1, 3, 2, 4).reshape(256, 256)
    grad_bias = final[34, :2].reshape(256)
    return layer_out, grad_feats, grad_weight, grad_bias


def solution(mesh):
    fine = Mesh(mesh.devices.reshape(4, 4, 4, 2, 2), AXES)
    blk, rep = ("x", "zl", "y"), ("zh", "c")
    return jax.shard_map(
        body,
        mesh=fine,
        in_specs=(
            P(blk, None),
            P(blk, rep, None, None),
            P(blk, rep),
            P(),
            P(),
            P(AXES, None),
        ),
        out_specs=(P(AXES, None), P(AXES, None), P(), P()),
        check_vma=False,
    )
```

```python
import math

import jax
import jax.numpy as jnp
from jax import lax
from jax.experimental import pallas as pl
from jax.experimental.pallas import tpu as pltpu
from jax.sharding import Mesh
from jax.sharding import PartitionSpec as P

AXES = ("x", "zl", "y", "zh", "c")
PLANE = ("x", "y")
GROUP = ("x", "y", "c")
TOP = lax.Precision.HIGH
F32 = jnp.float32
LIMIT = 10 * 1024 * 1024


def shift(value, axis, steps):
    count = lax.axis_size(axis)
    return lax.ppermute(value, axis, [(s, (s + steps) % count) for s in range(count)])


def ring(value, steps):
    pairs = []
    for s in range(8):
        for c in range(2):
            d = (s + (steps if abs(steps) == 1 or c == 0 else -steps)) % 8
            source, target = (s % 4) * 2 + s // 4, (d % 4) * 2 + d // 4
            pairs.append((source * 2 + c, target * 2 + c))
    return lax.ppermute(value, ("zl", "zh", "c"), pairs)


def exchange(value, axes):
    return lax.all_to_all(value, axes, 0, 0, tiled=True)


def vmem():
    return pl.BlockSpec(memory_space=pltpu.VMEM)


def smem():
    return pl.BlockSpec(memory_space=pltpu.SMEM)


def call(kernel, out_shape, specs, scratch=(), flops=0, moved=0):
    return pl.pallas_call(
        kernel,
        out_shape=out_shape,
        in_specs=specs,
        out_specs=jax.tree.map(lambda _: vmem(), out_shape),
        scratch_shapes=scratch,
        compiler_params=pltpu.CompilerParams(vmem_limit_bytes=LIMIT),
        cost_estimate=pl.CostEstimate(flops=flops, bytes_accessed=moved, transcendentals=0),
    )


def pack_kernel(where_ref, rows_ref, wanted_ref, out_ref):
    for h in range(2):

        @pl.when(where_ref[0] == h)
        def _():
            for b in range(4):
                half = rows_ref[128 * b : 128 * (b + 1), 128 * h : 128 * (h + 1)]
                out_ref[:, b] = half.reshape(16, 8, 128)

    out_ref[:, 4] = jnp.broadcast_to(wanted_ref[...].reshape(1, 1, 128), (16, 8, 128))


def row_of(where_ref, near_ref, far_ref, q, c, place):
    def asked(slot):
        source, core, k = slot // 8, slot // 4 % 2, slot % 4
        index_ref = far_ref if source else near_ref
        return index_ref[q, 16 * core + 8 * source + 4 * c + k]

    if place in (0, 8):
        return jnp.where(8 * where_ref[1] == place, asked(15), asked(place))
    return asked(place)


def gather_kernel(where_ref, near_ref, far_ref, table_ref, out_ref):
    def one(q, carry):
        for c in range(2):
            for slot in range(15):
                row = row_of(where_ref, near_ref, far_ref, q, c, slot)
                out_ref[q * 2 + c, slot] = table_ref[row]
        return carry

    lax.fori_loop(0, 16, one, 0)


def scatter_kernel(where_ref, near_ref, far_ref, got_ref, out_ref, even_ref, odd_ref):
    even_ref[...] = jnp.zeros_like(even_ref)
    odd_ref[...] = jnp.zeros_like(odd_ref)

    def one(q, carry):
        for slot in range(15):
            even_ref[row_of(where_ref, near_ref, far_ref, q, 0, slot)] += got_ref[q, 0, slot]
            odd_ref[row_of(where_ref, near_ref, far_ref, q, 1, slot)] += got_ref[q, 1, slot]
        return carry

    lax.fori_loop(0, 16, one, 0)
    sums = [jnp.sum(got_ref[:, 0, 15 + t] + got_ref[:, 1, 15 + t], axis=0) for t in range(3)]
    for plane in range(4):
        for part in range(3):
            out_ref[plane, part] = sums[part]
        rows = pl.ds(plane * 64, 64)
        out_ref[plane, 3:67] = even_ref[rows] + odd_ref[rows]


def unpack_kernel(home_ref, local_ref, feats_ref, weight_ref):
    for h in range(2):
        columns = slice(128 * h, 128 * (h + 1))
        feats_ref[:, columns] = home_ref[:, h, 0].reshape(128, 128) + local_ref[:, columns]
        weight_ref[:, columns] = home_ref[:, h, 1:].reshape(256, 128)


def dot(a, b):
    return lax.dot_general(
        a, b, (((1,), (0,)), ((), ())), precision=TOP, preferred_element_type=F32
    )


def dot_first(a, b):
    return lax.dot_general(
        a, b, (((0,), (0,)), ((), ())), precision=TOP, preferred_element_type=F32
    )


def dot_last(a, b):
    return lax.dot_general(
        a, b, (((1,), (1,)), ((), ())), precision=TOP, preferred_element_type=F32
    )


def middle_kernel(
    scale,
    where_ref,
    own_ref,
    beside_ref,
    across_ref,
    opposite_ref,
    rows_ref,
    got_ref,
    cot_ref,
    weight_ref,
    bias_ref,
    layer_ref,
    out_ref,
    local_ref,
):
    core, half = where_ref[0], where_ref[1]
    tiles = []
    for near_ref, far_ref in ((own_ref, beside_ref), (across_ref, opposite_ref)):
        for c in range(2):
            for k in range(4):
                tiles.append(jnp.where(core == c, near_ref[k], far_ref[k]))
    alone = jnp.where(half == 0, tiles[0], tiles[8])
    for j in (0, 8):
        tiles[j] = jnp.where(8 * half == j, tiles[15], tiles[j])
    tiles = jnp.concatenate(tiles[:15] + [alone], axis=1)
    rows = [
        jnp.concatenate([got_ref[:, h, j].reshape(128, 128) for h in range(2)], axis=1)
        for j in range(15)
    ]
    hidden = dot(tiles, jnp.concatenate(rows + [rows_ref[...]], axis=0))
    pre = dot(hidden, weight_ref[...]) + bias_ref[...]
    grow = jnp.exp(jnp.minimum(pre, 0.0))
    layer_ref[...] = jnp.where(pre > 0, pre, grow - 1.0)
    grad_pre = cot_ref[...] * jnp.where(pre > 0, 1.0, grow)
    grad_hidden = dot_last(grad_pre, weight_ref[...])
    terms = dot_first(tiles, grad_hidden)
    local_ref[...] = terms[1920:]
    grad_weight = dot_first(hidden, grad_pre) * scale
    grad_bias = jnp.sum(grad_pre, axis=0, keepdims=True) * scale
    row_ids = lax.broadcasted_iota(jnp.int32, (8, 128), 0)
    bias_tile = jnp.where(row_ids == 0, grad_bias[:, :128], 0.0)
    bias_tile = jnp.where(row_ids == 1, grad_bias[:, 128:], bias_tile)
    for h in range(2):
        columns = slice(128 * h, 128 * (h + 1))
        for j in range(15):
            out_ref[:, h, j] = terms[128 * j : 128 * (j + 1), columns].reshape(16, 8, 128)
        out_ref[:, h, 15:17] = grad_weight[:, columns].reshape(16, 2, 8, 128)
        out_ref[:, h, 17] = jnp.broadcast_to(bias_tile.reshape(1, 8, 128), (16, 8, 128))


def body(node_feats, operator_tiles, tile_cols, weight, layer_bias, cotangent):
    level = lax.axis_index("zl")
    half = lax.axis_index("zh")
    core = lax.axis_index("c")
    where = jnp.stack([core, half]).astype(jnp.int32)
    scale = 1.0 / math.sqrt(32768)

    mine = 2 * half + core

    def swapped(tiles, pairs):
        return lax.ppermute(tiles, ("zh", "c"), pairs)

    def tiles_for(block):
        return lax.dynamic_index_in_dim(operator_tiles, block, 0, keepdims=False)

    beside = swapped(tiles_for(2 * half + 1 - core), [(0, 1), (1, 0), (2, 3), (3, 2)])
    rows = lax.dynamic_slice_in_dim(node_feats, 128 * mine, 128, 0)

    asked = tile_cols.reshape(2, 8)
    owner = asked // 4
    spot = (owner // 16 * 4 + owner % 4) * 4 + asked % 4
    asked = jnp.mod(owner // 4 % 4 - level, 4) * 64 + spot
    asked = jnp.where(half == 0, asked, asked[::-1]).astype(F32).reshape(1, 16)
    asked_beside = shift(asked, "c", 1)
    wanted = jnp.where(
        core == 0,
        jnp.concatenate([asked, asked_beside], axis=1),
        jnp.concatenate([asked_beside, asked], axis=1),
    )
    wanted = jnp.pad(wanted, ((0, 0), (0, 96)))

    packed = call(
        pack_kernel,
        jax.ShapeDtypeStruct((16, 5, 8, 128), F32),
        [smem(), vmem(), vmem()],
        moved=1 << 20,
    )(where, node_feats, wanted)
    arrived = exchange(packed, PLANE)
    plane = arrived[:, :4].reshape(64, 8, 128)
    table = jnp.concatenate(
        [plane, ring(plane, -1), ring(plane, -2), ring(plane, 1)], axis=0
    )
    asked = arrived[:, 4, 0]
    index = (asked.astype(jnp.int32), shift(asked, "zh", 1).astype(jnp.int32))

    leaving = (tiles_for(2 * (1 - half) + core), tiles_for(2 * (1 - half) + 1 - core))
    table, leaving = lax.optimization_barrier((table, leaving))
    across = swapped(leaving[0], [(0, 2), (2, 0), (1, 3), (3, 1)])
    opposite = swapped(leaving[1], [(0, 3), (3, 0), (1, 2), (2, 1)])
    sent = call(
        gather_kernel,
        jax.ShapeDtypeStruct((32, 15, 8, 128), F32),
        [smem(), smem(), smem(), vmem()],
        moved=3 << 20,
    )(where, *index, table)
    got = exchange(sent, GROUP).reshape(16, 2, 15, 8, 128)
    def middle(*refs):
        middle_kernel(scale, *refs)

    layer_out, terms, local = call(
        middle,
        (
            jax.ShapeDtypeStruct((128, 256), F32),
            jax.ShapeDtypeStruct((16, 2, 18, 8, 128), F32),
            jax.ShapeDtypeStruct((128, 256), F32),
        ),
        [smem()] + [vmem()] * 9,
        flops=318767104 * 3,
        moved=6 << 20,
    )(
        where,
        tiles_for(mine),
        beside,
        across,
        opposite,
        rows,
        got,
        cotangent,
        weight,
        layer_bias.reshape(1, 256),
    )
    back = exchange(terms.reshape(32, 18, 8, 128), GROUP).reshape(16, 2, 18, 8, 128)
    sums = call(
        scatter_kernel,
        jax.ShapeDtypeStruct((4, 67, 8, 128), F32),
        [smem(), smem(), smem(), vmem()],
        scratch=[pltpu.VMEM((256, 8, 128), F32)] * 2,
        moved=4 << 20,
    )(where, *index, back)
    total = sums[0] + ring(sums[1], 1) + ring(sums[3], -1) + ring(sums[2], 2)
    by_owner = total[3:].reshape(16, 4, 8, 128)
    staying = lax.dynamic_slice_in_dim(by_owner, 2 * half, 2, 1).reshape(32, 8, 128)
    leaving = lax.dynamic_slice_in_dim(by_owner, 2 * (1 - half), 2, 1).reshape(32, 8, 128)
    final = jnp.concatenate([staying, total[:3]], axis=0) + shift(
        jnp.concatenate([leaving, total[:3]], axis=0), "zh", 1
    )
    home = exchange(
        jnp.concatenate(
            [
                final[:32, None],
                jnp.broadcast_to(final[None, 32:34], (32, 2, 8, 128)),
            ],
            axis=1,
        ),
        GROUP,
    ).reshape(16, 2, 3, 8, 128)
    grad_feats, grad_weight = call(
        unpack_kernel,
        (jax.ShapeDtypeStruct((128, 256), F32), jax.ShapeDtypeStruct((256, 256), F32)),
        [vmem(), vmem()],
        moved=1 << 20,
    )(home, local)
    grad_bias = final[34, :2].reshape(256)
    return layer_out, grad_feats, grad_weight, grad_bias


def solution(mesh):
    fine = Mesh(mesh.devices.reshape(4, 4, 4, 2, 2), AXES)
    blk, rep = ("x", "zl", "y"), ("zh", "c")
    return jax.shard_map(
        body,
        mesh=fine,
        in_specs=(
            P(blk, None),
            P(blk, rep, None, None),
            P(blk, rep),
            P(),
            P(),
            P(AXES, None),
        ),
        out_specs=(P(AXES, None), P(AXES, None), P(), P()),
        check_vma=False,
    )
```

```python
import math

import jax
import jax.numpy as jnp
from jax import lax
from jax.experimental import pallas as pl
from jax.experimental.pallas import tpu as pltpu
from jax.sharding import Mesh
from jax.sharding import PartitionSpec as P

AXES = ("x", "zl", "y", "zh", "c")
PLANE = ("x", "y")
GROUP = ("x", "y", "c")
TOP = lax.Precision.HIGH
F32 = jnp.float32
LIMIT = 10 * 1024 * 1024


def shift(value, axis, steps):
    count = lax.axis_size(axis)
    return lax.ppermute(value, axis, [(s, (s + steps) % count) for s in range(count)])


def ring(value, steps):
    pairs = []
    for s in range(8):
        for c in range(2):
            d = (s + (steps if abs(steps) == 1 or c == 0 else -steps)) % 8
            source, target = (s % 4) * 2 + s // 4, (d % 4) * 2 + d // 4
            pairs.append((source * 2 + c, target * 2 + c))
    return lax.ppermute(value, ("zl", "zh", "c"), pairs)


def exchange(value, axes):
    return lax.all_to_all(value, axes, 0, 0, tiled=True)


def vmem():
    return pl.BlockSpec(memory_space=pltpu.VMEM)


def smem():
    return pl.BlockSpec(memory_space=pltpu.SMEM)


def call(kernel, out_shape, specs, scratch=(), flops=0, moved=0):
    return pl.pallas_call(
        kernel,
        out_shape=out_shape,
        in_specs=specs,
        out_specs=jax.tree.map(lambda _: vmem(), out_shape),
        scratch_shapes=scratch,
        compiler_params=pltpu.CompilerParams(vmem_limit_bytes=LIMIT),
        cost_estimate=pl.CostEstimate(flops=flops, bytes_accessed=moved, transcendentals=0),
    )


def pack_kernel(rows_ref, wanted_ref, out_ref):
    for h in range(2):

        @pl.when(lax.axis_index("c") == h)
        def _():
            for b in range(4):
                half = rows_ref[128 * b : 128 * (b + 1), 128 * h : 128 * (h + 1)]
                out_ref[:, b] = half.reshape(16, 8, 128)

    out_ref[:, 4] = jnp.broadcast_to(wanted_ref[...].reshape(1, 1, 128), (16, 8, 128))


def row_of(near_ref, far_ref, q, c, place):
    def asked(slot):
        source, core, k = slot // 8, slot // 4 % 2, slot % 4
        index_ref = far_ref if source else near_ref
        return index_ref[q, 16 * core + 8 * source + 4 * c + k]

    if place in (0, 8):
        return jnp.where(8 * lax.axis_index("zh") == place, asked(15), asked(place))
    return asked(place)


def gather_kernel(near_ref, far_ref, table_ref, out_ref):
    def one(q, carry):
        for c in range(2):
            for slot in range(15):
                row = row_of(near_ref, far_ref, q, c, slot)
                out_ref[q * 2 + c, slot] = table_ref[row]
        return carry

    lax.fori_loop(0, 16, one, 0)


def scatter_kernel(near_ref, far_ref, got_ref, bias_ref, out_ref, even_ref, odd_ref):
    even_ref[...] = jnp.zeros_like(even_ref)
    odd_ref[...] = jnp.zeros_like(odd_ref)

    def one(q, carry):
        for slot in range(15):
            even_ref[row_of(near_ref, far_ref, q, 0, slot)] += got_ref[q, 0, slot]
            odd_ref[row_of(near_ref, far_ref, q, 1, slot)] += got_ref[q, 1, slot]
        return carry

    lax.fori_loop(0, 16, one, 0)
    sums = [jnp.sum(got_ref[:, 0, 15 + t] + got_ref[:, 1, 15 + t], axis=0) for t in range(2)]
    sums.append(bias_ref[...])
    for plane in range(4):
        for part in range(3):
            out_ref[plane, part] = sums[part]
        rows = pl.ds(plane * 64, 64)
        out_ref[plane, 3:67] = even_ref[rows] + odd_ref[rows]


def unpack_kernel(home_ref, local_ref, feats_ref, weight_ref, bias_ref):
    bias_ref[...] = jnp.sum(home_ref[:, 0, 3] + home_ref[:, 1, 3], axis=0)
    for h in range(2):
        columns = slice(128 * h, 128 * (h + 1))
        feats_ref[:, columns] = home_ref[:, h, 0].reshape(128, 128) + local_ref[:, columns]
        weight_ref[:, columns] = home_ref[:, h, 1:3].reshape(256, 128)


def dot(a, b):
    return lax.dot_general(
        a, b, (((1,), (0,)), ((), ())), precision=TOP, preferred_element_type=F32
    )


def dot_first(a, b):
    return lax.dot_general(
        a, b, (((0,), (0,)), ((), ())), precision=TOP, preferred_element_type=F32
    )


def dot_last(a, b):
    return lax.dot_general(
        a, b, (((1,), (1,)), ((), ())), precision=TOP, preferred_element_type=F32
    )


def middle_kernel(
    scale,
    own_ref,
    beside_ref,
    across_ref,
    opposite_ref,
    rows_ref,
    got_ref,
    cot_ref,
    weight_ref,
    layer_ref,
    out_ref,
    local_ref,
    bias_tile_ref,
):
    core, half = lax.axis_index("c"), lax.axis_index("zh")
    tiles = []
    for near_ref, far_ref in ((own_ref, beside_ref), (across_ref, opposite_ref)):
        for c in range(2):
            for k in range(4):
                tiles.append(jnp.where(core == c, near_ref[k], far_ref[k]))
    alone = jnp.where(half == 0, tiles[0], tiles[8])
    for j in (0, 8):
        tiles[j] = jnp.where(8 * half == j, tiles[15], tiles[j])
    tiles = jnp.concatenate(tiles[:15] + [alone], axis=1)
    rows = [
        jnp.concatenate([got_ref[:, h, j].reshape(128, 128) for h in range(2)], axis=1)
        for j in range(15)
    ]
    hidden = dot(tiles, jnp.concatenate(rows + [rows_ref[...]], axis=0))
    weight = weight_ref[:256]
    pre = dot(hidden, weight) + weight_ref[256:257]
    grow = jnp.exp(jnp.minimum(pre, 0.0))
    layer_ref[...] = jnp.where(pre > 0, pre, grow - 1.0)
    grad_pre = cot_ref[...] * jnp.where(pre > 0, 1.0, grow)
    grad_hidden = dot_last(grad_pre, weight)
    terms = dot_first(tiles, grad_hidden)
    local_ref[...] = terms[1920:]
    grad_weight = dot_first(hidden, grad_pre) * scale
    grad_bias = jnp.sum(grad_pre, axis=0, keepdims=True) * scale
    row_ids = lax.broadcasted_iota(jnp.int32, (8, 128), 0)
    bias_tile = jnp.where(row_ids == 0, grad_bias[:, :128], 0.0)
    bias_tile = jnp.where(row_ids == 1, grad_bias[:, 128:], bias_tile)
    bias_tile_ref[...] = bias_tile
    for h in range(2):
        columns = slice(128 * h, 128 * (h + 1))
        for j in range(15):
            out_ref[:, h, j] = terms[128 * j : 128 * (j + 1), columns].reshape(16, 8, 128)
        out_ref[:, h, 15:17] = grad_weight[:, columns].reshape(16, 2, 8, 128)


def body(node_feats, operator_tiles, tile_cols, weight, layer_bias, cotangent):
    level = lax.axis_index("zl")
    half = lax.axis_index("zh")
    core = lax.axis_index("c")
    scale = 1.0 / math.sqrt(32768)

    mine = 2 * half + core

    def swapped(tiles, pairs):
        return lax.ppermute(tiles, ("zh", "c"), pairs)

    def tiles_for(block):
        return lax.dynamic_index_in_dim(operator_tiles, block, 0, keepdims=False)

    beside = swapped(tiles_for(2 * half + 1 - core), [(0, 1), (1, 0), (2, 3), (3, 2)])
    rows = lax.dynamic_slice_in_dim(node_feats, 128 * mine, 128, 0)

    asked = tile_cols.reshape(2, 8)
    owner = asked // 4
    spot = (owner // 16 * 4 + owner % 4) * 4 + asked % 4
    asked = jnp.mod(owner // 4 % 4 - level, 4) * 64 + spot
    asked = jnp.where(half == 0, asked, asked[::-1]).astype(F32).reshape(1, 16)
    asked_beside = shift(asked, "c", 1)
    wanted = jnp.where(
        core == 0,
        jnp.concatenate([asked, asked_beside], axis=1),
        jnp.concatenate([asked_beside, asked], axis=1),
    )
    wanted = jnp.pad(wanted, ((0, 0), (0, 96)))

    packed = call(
        pack_kernel,
        jax.ShapeDtypeStruct((16, 5, 8, 128), F32),
        [vmem(), vmem()],
        moved=1 << 20,
    )(node_feats, wanted)
    arrived = exchange(packed, PLANE)
    plane = arrived[:, :4].reshape(64, 8, 128)
    table = jnp.concatenate(
        [plane, ring(plane, -1), ring(plane, -2), ring(plane, 1)], axis=0
    )
    asked = arrived[:, 4, 0]
    index = (asked.astype(jnp.int32), shift(asked, "zh", 1).astype(jnp.int32))

    leaving = (tiles_for(2 * (1 - half) + core), tiles_for(2 * (1 - half) + 1 - core))
    affine = jnp.concatenate([weight, jnp.broadcast_to(layer_bias, (8, 256))], axis=0)
    table, leaving, affine = lax.optimization_barrier((table, leaving, affine))
    across = swapped(leaving[0], [(0, 2), (2, 0), (1, 3), (3, 1)])
    opposite = swapped(leaving[1], [(0, 3), (3, 0), (1, 2), (2, 1)])
    sent = call(
        gather_kernel,
        jax.ShapeDtypeStruct((32, 15, 8, 128), F32),
        [smem(), smem(), vmem()],
        moved=3 << 20,
    )(*index, table)
    got = exchange(sent, GROUP).reshape(16, 2, 15, 8, 128)
    def middle(*refs):
        middle_kernel(scale, *refs)

    layer_out, terms, local, bias_part = call(
        middle,
        (
            jax.ShapeDtypeStruct((128, 256), F32),
            jax.ShapeDtypeStruct((16, 2, 17, 8, 128), F32),
            jax.ShapeDtypeStruct((128, 256), F32),
            jax.ShapeDtypeStruct((8, 128), F32),
        ),
        [vmem()] * 8,
        flops=318767104 * 3,
        moved=6 << 20,
    )(
        tiles_for(mine),
        beside,
        across,
        opposite,
        rows,
        got,
        cotangent,
        affine,
    )
    back = exchange(terms.reshape(32, 17, 8, 128), GROUP).reshape(16, 2, 17, 8, 128)
    sums = call(
        scatter_kernel,
        jax.ShapeDtypeStruct((4, 67, 8, 128), F32),
        [smem(), smem(), vmem(), vmem()],
        scratch=[pltpu.VMEM((256, 8, 128), F32)] * 2,
        moved=4 << 20,
    )(*index, back, bias_part)
    total = sums[0] + ring(sums[1], 1) + ring(sums[3], -1) + ring(sums[2], 2)
    by_owner = total[3:].reshape(16, 4, 8, 128)
    staying = lax.dynamic_slice_in_dim(by_owner, 2 * half, 2, 1).reshape(32, 8, 128)
    leaving = lax.dynamic_slice_in_dim(by_owner, 2 * (1 - half), 2, 1).reshape(32, 8, 128)
    final = jnp.concatenate([staying, total[:3]], axis=0) + shift(
        jnp.concatenate([leaving, total[:3]], axis=0), "zh", 1
    )
    home = exchange(
        jnp.concatenate(
            [
                final[:32, None],
                jnp.broadcast_to(final[None, 32:35], (32, 3, 8, 128)),
            ],
            axis=1,
        ),
        GROUP,
    ).reshape(16, 2, 4, 8, 128)
    grad_feats, grad_weight, bias_sum = call(
        unpack_kernel,
        (
            jax.ShapeDtypeStruct((128, 256), F32),
            jax.ShapeDtypeStruct((256, 256), F32),
            jax.ShapeDtypeStruct((8, 128), F32),
        ),
        [vmem(), vmem()],
        moved=1 << 20,
    )(home, local)
    grad_bias = bias_sum[:2].reshape(256)
    return layer_out, grad_feats, grad_weight, grad_bias


def solution(mesh):
    fine = Mesh(mesh.devices.reshape(4, 4, 4, 2, 2), AXES)
    blk, rep = ("x", "zl", "y"), ("zh", "c")
    return jax.shard_map(
        body,
        mesh=fine,
        in_specs=(
            P(blk, None),
            P(blk, rep, None, None),
            P(blk, rep),
            P(),
            P(),
            P(AXES, None),
        ),
        out_specs=(P(AXES, None), P(AXES, None), P(), P()),
        check_vma=False,
    )
```

```python
import math

import jax
import jax.numpy as jnp
from jax import lax
from jax.experimental import pallas as pl
from jax.experimental.pallas import tpu as pltpu
from jax.sharding import Mesh
from jax.sharding import PartitionSpec as P

AXES = ("x", "zl", "y", "zh", "c")
PLANE = ("x", "y")
GROUP = ("x", "y", "c")
TOP = lax.Precision.HIGH
F32 = jnp.float32
LIMIT = 10 * 1024 * 1024


def shift(value, axis, steps):
    count = lax.axis_size(axis)
    return lax.ppermute(value, axis, [(s, (s + steps) % count) for s in range(count)])


def ring(value, steps):
    pairs = []
    for s in range(8):
        for c in range(2):
            d = (s + (steps if abs(steps) == 1 or c == 0 else -steps)) % 8
            source, target = (s % 4) * 2 + s // 4, (d % 4) * 2 + d // 4
            pairs.append((source * 2 + c, target * 2 + c))
    return lax.ppermute(value, ("zl", "zh", "c"), pairs)


def exchange(value, axes):
    return lax.all_to_all(value, axes, 0, 0, tiled=True)


def vmem():
    return pl.BlockSpec(memory_space=pltpu.VMEM)


def smem():
    return pl.BlockSpec(memory_space=pltpu.SMEM)


def call(kernel, out_shape, specs, scratch=(), flops=0, moved=0):
    return pl.pallas_call(
        kernel,
        out_shape=out_shape,
        in_specs=specs,
        out_specs=jax.tree.map(lambda _: vmem(), out_shape),
        scratch_shapes=scratch,
        compiler_params=pltpu.CompilerParams(vmem_limit_bytes=LIMIT),
        cost_estimate=pl.CostEstimate(flops=flops, bytes_accessed=moved, transcendentals=0),
    )


def pack_kernel(rows_ref, wanted_ref, out_ref):
    for h in range(2):

        @pl.when(lax.axis_index("c") == h)
        def _():
            for b in range(4):
                half = rows_ref[128 * b : 128 * (b + 1), 128 * h : 128 * (h + 1)]
                out_ref[:, b] = half.reshape(16, 8, 128)

    out_ref[:, 4] = jnp.broadcast_to(wanted_ref[...].reshape(1, 1, 128), (16, 8, 128))


def row_of(near_ref, far_ref, q, c, place):
    def asked(slot):
        source, core, k = slot // 8, slot // 4 % 2, slot % 4
        index_ref = far_ref if source else near_ref
        return index_ref[q, 16 * core + 8 * source + 4 * c + k]

    if place in (0, 8):
        return jnp.where(8 * lax.axis_index("zh") == place, asked(15), asked(place))
    return asked(place)


def gather_kernel(near_ref, far_ref, table_ref, out_ref):
    def one(q, carry):
        for c in range(2):
            for slot in range(15):
                row = row_of(near_ref, far_ref, q, c, slot)
                out_ref[q * 2 + c, slot] = table_ref[row]
        return carry

    lax.fori_loop(0, 16, one, 0)


def scatter_kernel(near_ref, far_ref, got_ref, bias_ref, out_ref, even_ref, odd_ref):
    even_ref[...] = jnp.zeros_like(even_ref)
    odd_ref[...] = jnp.zeros_like(odd_ref)

    def one(q, carry):
        for slot in range(15):
            even_ref[row_of(near_ref, far_ref, q, 0, slot)] += got_ref[q, 0, slot]
            odd_ref[row_of(near_ref, far_ref, q, 1, slot)] += got_ref[q, 1, slot]
        return carry

    lax.fori_loop(0, 16, one, 0)
    sums = [jnp.sum(got_ref[:, 0, 15 + t] + got_ref[:, 1, 15 + t], axis=0) for t in range(2)]
    sums.append(bias_ref[...])
    for plane in range(4):
        for part in range(3):
            out_ref[plane, part] = sums[part]
        rows = pl.ds(plane * 64, 64)
        out_ref[plane, 3:67] = even_ref[rows] + odd_ref[rows]


def unpack_kernel(home_ref, local_ref, feats_ref, weight_ref, bias_ref):
    total = jnp.sum(home_ref[:, 0, 3] + home_ref[:, 1, 3], axis=0)
    bias_ref[:, :128] = total[0:1]
    bias_ref[:, 128:] = total[1:2]
    for h in range(2):
        columns = slice(128 * h, 128 * (h + 1))
        feats_ref[:, columns] = home_ref[:, h, 0].reshape(128, 128) + local_ref[:, columns]
        weight_ref[:, columns] = home_ref[:, h, 1:3].reshape(256, 128)


def dot(a, b):
    return lax.dot_general(
        a, b, (((1,), (0,)), ((), ())), precision=TOP, preferred_element_type=F32
    )


def dot_first(a, b):
    return lax.dot_general(
        a, b, (((0,), (0,)), ((), ())), precision=TOP, preferred_element_type=F32
    )


def dot_last(a, b):
    return lax.dot_general(
        a, b, (((1,), (1,)), ((), ())), precision=TOP, preferred_element_type=F32
    )


def middle_kernel(
    scale,
    own_ref,
    beside_ref,
    across_ref,
    opposite_ref,
    rows_ref,
    got_ref,
    cot_ref,
    weight_ref,
    layer_ref,
    out_ref,
    local_ref,
    bias_tile_ref,
):
    core, half = lax.axis_index("c"), lax.axis_index("zh")
    tiles = []
    for near_ref, far_ref in ((own_ref, beside_ref), (across_ref, opposite_ref)):
        for c in range(2):
            for k in range(4):
                tiles.append(jnp.where(core == c, near_ref[k], far_ref[k]))
    alone = jnp.where(half == 0, tiles[0], tiles[8])
    for j in (0, 8):
        tiles[j] = jnp.where(8 * half == j, tiles[15], tiles[j])
    tiles = jnp.concatenate(tiles[:15] + [alone], axis=1)
    rows = [
        jnp.concatenate([got_ref[:, h, j].reshape(128, 128) for h in range(2)], axis=1)
        for j in range(15)
    ]
    hidden = dot(tiles, jnp.concatenate(rows + [rows_ref[...]], axis=0))
    weight = weight_ref[:256]
    pre = dot(hidden, weight) + weight_ref[256:257]
    grow = jnp.exp(jnp.minimum(pre, 0.0))
    layer_ref[...] = jnp.where(pre > 0, pre, grow - 1.0)
    grad_pre = cot_ref[...] * jnp.where(pre > 0, 1.0, grow)
    grad_hidden = dot_last(grad_pre, weight)
    terms = dot_first(tiles, grad_hidden)
    local_ref[...] = terms[1920:]
    grad_weight = dot_first(hidden, grad_pre) * scale
    grad_bias = jnp.sum(grad_pre, axis=0, keepdims=True) * scale
    row_ids = lax.broadcasted_iota(jnp.int32, (8, 128), 0)
    bias_tile = jnp.where(row_ids == 0, grad_bias[:, :128], 0.0)
    bias_tile = jnp.where(row_ids == 1, grad_bias[:, 128:], bias_tile)
    bias_tile_ref[...] = bias_tile
    for h in range(2):
        columns = slice(128 * h, 128 * (h + 1))
        for j in range(15):
            out_ref[:, h, j] = terms[128 * j : 128 * (j + 1), columns].reshape(16, 8, 128)
        out_ref[:, h, 15:17] = grad_weight[:, columns].reshape(16, 2, 8, 128)


def body(node_feats, operator_tiles, tile_cols, weight, layer_bias, cotangent):
    level = lax.axis_index("zl")
    half = lax.axis_index("zh")
    core = lax.axis_index("c")
    scale = 1.0 / math.sqrt(32768)

    mine = 2 * half + core

    def swapped(tiles, pairs):
        return lax.ppermute(tiles, ("zh", "c"), pairs)

    def tiles_for(block):
        return lax.dynamic_index_in_dim(operator_tiles, block, 0, keepdims=False)

    beside = swapped(tiles_for(2 * half + 1 - core), [(0, 1), (1, 0), (2, 3), (3, 2)])
    rows = lax.dynamic_slice_in_dim(node_feats, 128 * mine, 128, 0)

    asked = tile_cols.reshape(2, 8)
    owner = asked // 4
    spot = (owner // 16 * 4 + owner % 4) * 4 + asked % 4
    asked = jnp.mod(owner // 4 % 4 - level, 4) * 64 + spot
    asked = jnp.where(half == 0, asked, asked[::-1]).astype(F32).reshape(1, 16)
    asked_beside = shift(asked, "c", 1)
    wanted = jnp.where(
        core == 0,
        jnp.concatenate([asked, asked_beside], axis=1),
        jnp.concatenate([asked_beside, asked], axis=1),
    )
    wanted = jnp.pad(wanted, ((0, 0), (0, 96)))

    packed = call(
        pack_kernel,
        jax.ShapeDtypeStruct((16, 5, 8, 128), F32),
        [vmem(), vmem()],
        moved=1 << 20,
    )(node_feats, wanted)
    arrived = exchange(packed, PLANE)
    plane = arrived[:, :4].reshape(64, 8, 128)
    plane, asked = lax.optimization_barrier((plane, arrived[:, 4, 0]))
    asked_far = shift(asked, "zh", 1)
    index = (asked.astype(jnp.int32), asked_far.astype(jnp.int32))
    table = jnp.concatenate(
        [plane, ring(plane, -1), ring(plane, -2), ring(plane, 1)], axis=0
    )
    leaving = (tiles_for(2 * (1 - half) + core), tiles_for(2 * (1 - half) + 1 - core))
    affine = jnp.concatenate([weight, jnp.broadcast_to(layer_bias, (8, 256))], axis=0)
    table, leaving, affine = lax.optimization_barrier((table, leaving, affine))
    across = swapped(leaving[0], [(0, 2), (2, 0), (1, 3), (3, 1)])
    opposite = swapped(leaving[1], [(0, 3), (3, 0), (1, 2), (2, 1)])
    sent = call(
        gather_kernel,
        jax.ShapeDtypeStruct((32, 15, 8, 128), F32),
        [smem(), smem(), vmem()],
        moved=3 << 20,
    )(*index, table)
    got = exchange(sent, GROUP).reshape(16, 2, 15, 8, 128)
    def middle(*refs):
        middle_kernel(scale, *refs)

    layer_out, terms, local, bias_part = call(
        middle,
        (
            jax.ShapeDtypeStruct((128, 256), F32),
            jax.ShapeDtypeStruct((16, 2, 17, 8, 128), F32),
            jax.ShapeDtypeStruct((128, 256), F32),
            jax.ShapeDtypeStruct((8, 128), F32),
        ),
        [vmem()] * 8,
        flops=318767104 * 3,
        moved=6 << 20,
    )(
        tiles_for(mine),
        beside,
        across,
        opposite,
        rows,
        got,
        cotangent,
        affine,
    )
    back = exchange(terms.reshape(32, 17, 8, 128), GROUP).reshape(16, 2, 17, 8, 128)
    sums = call(
        scatter_kernel,
        jax.ShapeDtypeStruct((4, 67, 8, 128), F32),
        [smem(), smem(), vmem(), vmem()],
        scratch=[pltpu.VMEM((256, 8, 128), F32)] * 2,
        moved=4 << 20,
    )(*index, back, bias_part)
    total = sums[0] + ring(sums[1], 1) + ring(sums[3], -1) + ring(sums[2], 2)
    by_owner = total[3:].reshape(16, 4, 8, 128)
    staying = lax.dynamic_slice_in_dim(by_owner, 2 * half, 2, 1).reshape(32, 8, 128)
    leaving = lax.dynamic_slice_in_dim(by_owner, 2 * (1 - half), 2, 1).reshape(32, 8, 128)
    final = jnp.concatenate([staying, total[:3]], axis=0) + shift(
        jnp.concatenate([leaving, total[:3]], axis=0), "zh", 1
    )
    home = exchange(
        jnp.concatenate(
            [
                final[:32, None],
                jnp.broadcast_to(final[None, 32:35], (32, 3, 8, 128)),
            ],
            axis=1,
        ),
        GROUP,
    ).reshape(16, 2, 4, 8, 128)
    grad_feats, grad_weight, bias_sum = call(
        unpack_kernel,
        (
            jax.ShapeDtypeStruct((128, 256), F32),
            jax.ShapeDtypeStruct((256, 256), F32),
            jax.ShapeDtypeStruct((1, 256), F32),
        ),
        [vmem(), vmem()],
        moved=1 << 20,
    )(home, local)
    grad_bias = bias_sum.reshape(256)
    return layer_out, grad_feats, grad_weight, grad_bias


def solution(mesh):
    fine = Mesh(mesh.devices.reshape(4, 4, 4, 2, 2), AXES)
    blk, rep = ("x", "zl", "y"), ("zh", "c")
    return jax.shard_map(
        body,
        mesh=fine,
        in_specs=(
            P(blk, None),
            P(blk, rep, None, None),
            P(blk, rep),
            P(),
            P(),
            P(AXES, None),
        ),
        out_specs=(P(AXES, None), P(AXES, None), P(), P()),
        check_vma=False,
    )
```

```python
import math

import jax
import jax.numpy as jnp
from jax import lax
from jax.experimental import pallas as pl
from jax.experimental.pallas import tpu as pltpu
from jax.sharding import Mesh
from jax.sharding import PartitionSpec as P

AXES = ("x", "zl", "y", "zh", "c")
PLANE = ("x", "y")
GROUP = ("x", "y", "c")
TOP = lax.Precision.HIGH
F32 = jnp.float32
LIMIT = 10 * 1024 * 1024


def shift(value, axis, steps):
    count = lax.axis_size(axis)
    return lax.ppermute(value, axis, [(s, (s + steps) % count) for s in range(count)])


def ring(value, steps):
    pairs = []
    for s in range(8):
        for c in range(2):
            d = (s + (steps if abs(steps) == 1 or c == 0 else -steps)) % 8
            source, target = (s % 4) * 2 + s // 4, (d % 4) * 2 + d // 4
            pairs.append((source * 2 + c, target * 2 + c))
    return lax.ppermute(value, ("zl", "zh", "c"), pairs)


def exchange(value, axes):
    return lax.all_to_all(value, axes, 0, 0, tiled=True)


def vmem():
    return pl.BlockSpec(memory_space=pltpu.VMEM)


def smem():
    return pl.BlockSpec(memory_space=pltpu.SMEM)


def call(kernel, out_shape, specs, scratch=(), flops=0, moved=0):
    return pl.pallas_call(
        kernel,
        out_shape=out_shape,
        in_specs=specs,
        out_specs=jax.tree.map(lambda _: vmem(), out_shape),
        scratch_shapes=scratch,
        compiler_params=pltpu.CompilerParams(vmem_limit_bytes=LIMIT),
        cost_estimate=pl.CostEstimate(flops=flops, bytes_accessed=moved, transcendentals=0),
    )


def pack_kernel(rows_ref, wanted_ref, out_ref):
    for h in range(2):

        @pl.when(lax.axis_index("c") == h)
        def _():
            for b in range(4):
                half = rows_ref[128 * b : 128 * (b + 1), 128 * h : 128 * (h + 1)]
                out_ref[:, b] = half.reshape(16, 8, 128)

    out_ref[:, 4] = jnp.broadcast_to(wanted_ref[...].reshape(1, 1, 128), (16, 8, 128))


def row_of(near_ref, far_ref, q, c, place):
    def asked(slot):
        source, core, k = slot // 8, slot // 4 % 2, slot % 4
        index_ref = far_ref if source else near_ref
        return index_ref[q, 16 * core + 8 * source + 4 * c + k]

    if place in (0, 8):
        return jnp.where(8 * lax.axis_index("zh") == place, asked(15), asked(place))
    return asked(place)


def gather_kernel(near_ref, far_ref, table_ref, out_ref):
    def one(q, carry):
        for c in range(2):
            for slot in range(15):
                row = row_of(near_ref, far_ref, q, c, slot)
                out_ref[q * 2 + c, slot] = table_ref[row]
        return carry

    lax.fori_loop(0, 16, one, 0)


def scatter_kernel(near_ref, far_ref, got_ref, bias_ref, out_ref, even_ref, odd_ref):
    even_ref[...] = jnp.zeros_like(even_ref)
    odd_ref[...] = jnp.zeros_like(odd_ref)

    def one(q, carry):
        for slot in range(15):
            even_ref[row_of(near_ref, far_ref, q, 0, slot)] += got_ref[q, 0, slot]
            odd_ref[row_of(near_ref, far_ref, q, 1, slot)] += got_ref[q, 1, slot]
        return carry

    lax.fori_loop(0, 16, one, 0)
    sums = [jnp.sum(got_ref[:, 0, 15 + t] + got_ref[:, 1, 15 + t], axis=0) for t in range(2)]
    sums.append(bias_ref[...])
    for plane in range(4):
        for part in range(3):
            out_ref[plane, part] = sums[part]
        rows = pl.ds(plane * 64, 64)
        out_ref[plane, 3:67] = even_ref[rows] + odd_ref[rows]


def unpack_kernel(home_ref, local_ref, feats_ref, weight_ref, bias_ref):
    total = jnp.sum(home_ref[:, 0, 3] + home_ref[:, 1, 3], axis=0)
    bias_ref[:, :128] = total[0:1]
    bias_ref[:, 128:] = total[1:2]
    for h in range(2):
        columns = slice(128 * h, 128 * (h + 1))
        feats_ref[:, columns] = home_ref[:, h, 0].reshape(128, 128) + local_ref[:, columns]
        weight_ref[:, columns] = home_ref[:, h, 1:3].reshape(256, 128)


def dot(a, b):
    return lax.dot_general(
        a, b, (((1,), (0,)), ((), ())), precision=TOP, preferred_element_type=F32
    )


def dot_first(a, b):
    return lax.dot_general(
        a, b, (((0,), (0,)), ((), ())), precision=TOP, preferred_element_type=F32
    )


def dot_last(a, b):
    return lax.dot_general(
        a, b, (((1,), (1,)), ((), ())), precision=TOP, preferred_element_type=F32
    )


def middle_kernel(
    scale,
    own_ref,
    beside_ref,
    early_ref,
    across_ref,
    opposite_ref,
    rows_ref,
    got_ref,
    cot_ref,
    weight_ref,
    layer_ref,
    out_ref,
    local_ref,
    bias_tile_ref,
):
    core, half = lax.axis_index("c"), lax.axis_index("zh")
    tiles = []
    across = [early_ref[0]] + [across_ref[k] for k in range(3)]
    near = [own_ref[k] for k in range(4)] + across
    far = [beside_ref[k] for k in range(4)] + [opposite_ref[k] for k in range(4)]
    for source in range(2):
        for c in range(2):
            for k in range(4 * source, 4 * source + 4):
                tiles.append(jnp.where(core == c, near[k], far[k]))
    alone = jnp.where(half == 0, tiles[0], tiles[8])
    for j in (0, 8):
        tiles[j] = jnp.where(8 * half == j, tiles[15], tiles[j])
    tiles = jnp.concatenate(tiles[:15] + [alone], axis=1)
    rows = [
        jnp.concatenate([got_ref[:, h, j].reshape(128, 128) for h in range(2)], axis=1)
        for j in range(15)
    ]
    hidden = dot(tiles, jnp.concatenate(rows + [rows_ref[...]], axis=0))
    weight = weight_ref[:256]
    pre = dot(hidden, weight) + weight_ref[256:257]
    grow = jnp.exp(jnp.minimum(pre, 0.0))
    layer_ref[...] = jnp.where(pre > 0, pre, grow - 1.0)
    grad_pre = cot_ref[...] * jnp.where(pre > 0, 1.0, grow)
    grad_hidden = dot_last(grad_pre, weight)
    terms = dot_first(tiles, grad_hidden)
    local_ref[...] = terms[1920:]
    grad_weight = dot_first(hidden, grad_pre) * scale
    grad_bias = jnp.sum(grad_pre, axis=0, keepdims=True) * scale
    row_ids = lax.broadcasted_iota(jnp.int32, (8, 128), 0)
    bias_tile = jnp.where(row_ids == 0, grad_bias[:, :128], 0.0)
    bias_tile = jnp.where(row_ids == 1, grad_bias[:, 128:], bias_tile)
    bias_tile_ref[...] = bias_tile
    for h in range(2):
        columns = slice(128 * h, 128 * (h + 1))
        for j in range(15):
            out_ref[:, h, j] = terms[128 * j : 128 * (j + 1), columns].reshape(16, 8, 128)
        out_ref[:, h, 15:17] = grad_weight[:, columns].reshape(16, 2, 8, 128)


def body(node_feats, operator_tiles, tile_cols, weight, layer_bias, cotangent):
    level = lax.axis_index("zl")
    half = lax.axis_index("zh")
    core = lax.axis_index("c")
    scale = 1.0 / math.sqrt(32768)

    mine = 2 * half + core

    def swapped(tiles, pairs):
        return lax.ppermute(tiles, ("zh", "c"), pairs)

    def tiles_for(block):
        return lax.dynamic_index_in_dim(operator_tiles, block, 0, keepdims=False)

    beside = swapped(tiles_for(2 * half + 1 - core), [(0, 1), (1, 0), (2, 3), (3, 2)])
    rows = lax.dynamic_slice_in_dim(node_feats, 128 * mine, 128, 0)

    asked = tile_cols.reshape(2, 8)
    owner = asked // 4
    spot = (owner // 16 * 4 + owner % 4) * 4 + asked % 4
    asked = jnp.mod(owner // 4 % 4 - level, 4) * 64 + spot
    asked = jnp.where(half == 0, asked, asked[::-1]).astype(F32).reshape(1, 16)
    asked_beside = shift(asked, "c", 1)
    wanted = jnp.where(
        core == 0,
        jnp.concatenate([asked, asked_beside], axis=1),
        jnp.concatenate([asked_beside, asked], axis=1),
    )
    wanted = jnp.pad(wanted, ((0, 0), (0, 96)))

    packed = call(
        pack_kernel,
        jax.ShapeDtypeStruct((16, 5, 8, 128), F32),
        [vmem(), vmem()],
        moved=1 << 20,
    )(node_feats, wanted)
    arrived = exchange(packed, PLANE)
    plane = arrived[:, :4].reshape(64, 8, 128)
    plane, asked = lax.optimization_barrier((plane, arrived[:, 4, 0]))
    asked_far = shift(asked, "zh", 1)
    index = (asked.astype(jnp.int32), asked_far.astype(jnp.int32))
    table = jnp.concatenate(
        [plane, ring(plane, -1), ring(plane, -2), ring(plane, 1)], axis=0
    )
    leaving = (tiles_for(2 * (1 - half) + core), tiles_for(2 * (1 - half) + 1 - core))
    affine = jnp.concatenate([weight, jnp.broadcast_to(layer_bias, (8, 256))], axis=0)
    over = [(0, 2), (2, 0), (1, 3), (3, 1)]
    early = swapped(leaving[0][:1], over)
    leaving = (leaving[0][1:], leaving[1])
    table, leaving, affine = lax.optimization_barrier((table, leaving, affine))
    across = swapped(leaving[0], [(0, 2), (2, 0), (1, 3), (3, 1)])
    opposite = swapped(leaving[1], [(0, 3), (3, 0), (1, 2), (2, 1)])
    sent = call(
        gather_kernel,
        jax.ShapeDtypeStruct((32, 15, 8, 128), F32),
        [smem(), smem(), vmem()],
        moved=3 << 20,
    )(*index, table)
    sent, early = lax.optimization_barrier((sent, early))
    got = exchange(sent, GROUP).reshape(16, 2, 15, 8, 128)
    def middle(*refs):
        middle_kernel(scale, *refs)

    layer_out, terms, local, bias_part = call(
        middle,
        (
            jax.ShapeDtypeStruct((128, 256), F32),
            jax.ShapeDtypeStruct((16, 2, 17, 8, 128), F32),
            jax.ShapeDtypeStruct((128, 256), F32),
            jax.ShapeDtypeStruct((8, 128), F32),
        ),
        [vmem()] * 9,
        flops=318767104 * 3,
        moved=6 << 20,
    )(
        tiles_for(mine),
        beside,
        early,
        across,
        opposite,
        rows,
        got,
        cotangent,
        affine,
    )
    back = exchange(terms.reshape(32, 17, 8, 128), GROUP).reshape(16, 2, 17, 8, 128)
    sums = call(
        scatter_kernel,
        jax.ShapeDtypeStruct((4, 67, 8, 128), F32),
        [smem(), smem(), vmem(), vmem()],
        scratch=[pltpu.VMEM((256, 8, 128), F32)] * 2,
        moved=4 << 20,
    )(*index, back, bias_part)
    total = sums[0] + ring(sums[1], 1) + ring(sums[3], -1) + ring(sums[2], 2)
    by_owner = total[3:].reshape(16, 4, 8, 128)
    staying = lax.dynamic_slice_in_dim(by_owner, 2 * half, 2, 1).reshape(32, 8, 128)
    leaving = lax.dynamic_slice_in_dim(by_owner, 2 * (1 - half), 2, 1).reshape(32, 8, 128)
    final = jnp.concatenate([staying, total[:3]], axis=0) + shift(
        jnp.concatenate([leaving, total[:3]], axis=0), "zh", 1
    )
    home = exchange(
        jnp.concatenate(
            [
                final[:32, None],
                jnp.broadcast_to(final[None, 32:35], (32, 3, 8, 128)),
            ],
            axis=1,
        ),
        GROUP,
    ).reshape(16, 2, 4, 8, 128)
    grad_feats, grad_weight, bias_sum = call(
        unpack_kernel,
        (
            jax.ShapeDtypeStruct((128, 256), F32),
            jax.ShapeDtypeStruct((256, 256), F32),
            jax.ShapeDtypeStruct((1, 256), F32),
        ),
        [vmem(), vmem()],
        moved=1 << 20,
    )(home, local)
    grad_bias = bias_sum.reshape(256)
    return layer_out, grad_feats, grad_weight, grad_bias


def solution(mesh):
    fine = Mesh(mesh.devices.reshape(4, 4, 4, 2, 2), AXES)
    blk, rep = ("x", "zl", "y"), ("zh", "c")
    return jax.shard_map(
        body,
        mesh=fine,
        in_specs=(
            P(blk, None),
            P(blk, rep, None, None),
            P(blk, rep),
            P(),
            P(),
            P(AXES, None),
        ),
        out_specs=(P(AXES, None), P(AXES, None), P(), P()),
        check_vma=False,
    )
```
